256 devices in a mesh: group: 8 (over y, core), dev: 32 (over z, x).
Axes of the slice: x: 4, y: 4, z: 8, core: 2. Of those that a mesh axis runs over, the one named last changes fastest.
Arguments:
- points: float32 [440, 131072], P(None, ('group', 'dev')), may hold values from -6 to 6
- residual: float32 [147, 131072], P(None, ('group', 'dev')), may hold values from -6 to 6
- coeffs: float32 [147, 131072], P(None, ('group', 'dev')), may hold values from -3 to 3
- owners: int32 [2], replicated, may hold values from 0 to 255
- offsets: int32 [2], replicated, may hold values from 0 to 256
Outputs:
- new_residual: float32 [147, 131072], P(None, ('group', 'dev'))
- new_coeffs: float32 [147, 131072], P(None, ('group', 'dev'))
The draws below stay inside these ranges and needn't reach their ends.
All inputs are finite; a program needn't handle non-finite values.
Results may differ from the reference program's by a relative error of at most 0.0003.
Values sent between devices are 32-bit elements; how exact they have to be, the bound alone decides.
No kernel may reach another device: no remote copies, remote signals or barrier semaphores. Data moves between devices by JAX's collectives and lax.ppermute only.
A program may use at most 64 MiB of HBM per device.

```python
import jax
import jax.numpy as jnp
from jax import lax

FEATURES = 440
CLASSES = 147
BLOCK = 256
ROWS_DEV = 512
NPTS = 131072
N_GROUP = 8
N_DEV = 32


def block_scale(key, dims, cuts, smallest, high):
    factor_of, own = 1.0, jax.random.fold_in(key, 6)
    for axis_at, shards_of in cuts:
        heights = jnp.exp(jax.random.uniform(jax.random.fold_in(own, axis_at), (shards_of,), jnp.float32, smallest / len(cuts), high / len(cuts)))
        factor_of = factor_of * jnp.repeat(heights, dims[axis_at] // shards_of).reshape([-1 if axis == axis_at else 1 for axis in range(len(dims))])
    return factor_of


def scatter_about(rng, shape, deviation, most, shards=(), kind=jnp.bfloat16):
    array = jax.random.normal(rng, shape, jnp.float32) * deviation
    if len(shards) > 0:
        array = block_scale(rng, shape, shards, -0.22, 0.18) * array
    return jnp.clip(array, min=-most, max=most).astype(kind)


def setup_inputs(seed: int = 0) -> dict:
    arg_keys = jax.random.split(jax.random.key(seed), 6)
    points = scatter_about(arg_keys[0], (FEATURES, NPTS), 1.0, 6.0, ((1, 256),), jnp.float32)
    residual = scatter_about(arg_keys[1], (CLASSES, NPTS), 1.0, 6.0, ((1, 256),), jnp.float32)
    coeffs = scatter_about(arg_keys[2], (CLASSES, NPTS), 0.5, 3.0, ((1, 256),), jnp.float32)
    owners = jax.random.randint(arg_keys[3], (2,), 0, N_GROUP * N_DEV).astype(jnp.int32)
    offsets = jax.random.randint(arg_keys[4], (2,), 0, ROWS_DEV - BLOCK + 1).astype(jnp.int32)
    return dict(points=points, residual=residual, coeffs=coeffs, owners=owners, offsets=offsets)


ridge = 2.0
step_norm = 1.5

def kernel_tile(cols, block):
    cross = lax.dot_general(block.astype(jnp.float32), cols.astype(jnp.float32), (((0,), (0,)), ((), ())), precision=lax.Precision.HIGHEST, preferred_element_type=jnp.float32)
    dist = lax.optimization_barrier(jnp.sum(block * block, axis=0))[:, None] + lax.optimization_barrier(jnp.sum(cols * cols, axis=0))[None, :] - 2.0 * cross
    return jnp.exp(-dist / cols.shape[0])

def precondition(grad, block):
    gram = kernel_tile(block, block) + ridge * jnp.eye(block.shape[1], dtype=jnp.float32)
    lower = jnp.linalg.cholesky(gram)
    inner = lax.linalg.triangular_solve(lower, grad.T, left_side=True, lower=True)
    solved = lax.linalg.triangular_solve(lower, inner, left_side=True, lower=True, transpose_a=True)
    scale = step_norm / jnp.sqrt(jnp.mean(grad * grad) + 1e-06)
    return scale * solved.T

def reference(points, residual, coeffs, owners, offsets):
    count = NPTS // ROWS_DEV
    for step in range(2):
        start = (owners[step] * ROWS_DEV + offsets[step]).astype(jnp.int32)
        block = lax.dynamic_slice_in_dim(points, start, BLOCK, 1)

        def accumulate(total, index):
            first = (index * ROWS_DEV).astype(jnp.int32)
            cols = lax.dynamic_slice_in_dim(points, first, ROWS_DEV, 1)
            resid = lax.dynamic_slice_in_dim(residual, first, ROWS_DEV, 1)
            tile = kernel_tile(cols, block)
            part = lax.dot_general(resid.astype(jnp.float32), tile.astype(jnp.float32), (((1,), (1,)), ((), ())), precision=lax.Precision.HIGHEST, preferred_element_type=jnp.float32)
            return (total + part, None)
        grad, _ = lax.scan(accumulate, jnp.zeros((CLASSES, BLOCK), jnp.float32), jnp.arange(count, dtype=jnp.int32))
        delta = precondition(grad, block)

        def update(index):
            first = (index * ROWS_DEV).astype(jnp.int32)
            cols = lax.dynamic_slice_in_dim(points, first, ROWS_DEV, 1)
            resid = lax.dynamic_slice_in_dim(residual, first, ROWS_DEV, 1)
            tile = kernel_tile(cols, block)
            return resid - jnp.dot(delta.astype(jnp.float32), tile.astype(jnp.float32), precision=lax.Precision.HIGHEST, preferred_element_type=jnp.float32)
        pieces = lax.map(update, jnp.arange(count, dtype=jnp.int32))
        residual = jnp.transpose(pieces, (1, 0, 2)).reshape(CLASSES, NPTS)
        current = lax.dynamic_slice_in_dim(coeffs, start, BLOCK, 1)
        coeffs = lax.dynamic_update_slice_in_dim(coeffs, current + delta, start, 1)
    return (residual, coeffs)
```

```python
import functools
import itertools

import jax
import jax.numpy as jnp
from jax import lax
from jax.experimental import pallas as pl
from jax.experimental.pallas import tpu as pltpu
from jax.sharding import PartitionSpec as P

BLOCK = 256
LANES = 128
AXES = ("group", "dev")

VMEM_LIMIT = 24 << 20
SWEEP_FLOPS = 4_000_000_000

ridge = 2.0
step_norm = 1.5

VMEM = pl.BlockSpec(memory_space=pltpu.VMEM)
SMEM = pl.BlockSpec(memory_space=pltpu.SMEM)


def rings():
    ys, cores, zs, xs = range(4), range(2), range(8), range(4)
    at = lambda y, c, z, x: (y * 2 + c) * 32 + z * 4 + x
    planes = [[at(y, c, z, x) for y, x in itertools.product(ys, xs)] for c, z in itertools.product(cores, zs)]
    lines = [[at(y, c, z, x) for z in zs] for y, c, x in itertools.product(ys, cores, xs)]
    partners = [(at(y, c, z, x), at(y, 1 - c, z, x)) for y, c, z, x in itertools.product(ys, cores, zs, xs)]
    return planes, lines, partners


PLANES, LINES, PARTNERS = rings()


def swap(value):
    return lax.ppermute(value, AXES, PARTNERS)


def exchange(value, groups):
    return lax.all_to_all(value, AXES, 0, 0, tiled=True, axis_index_groups=groups)


def scatter_sum(value, groups):
    n = len(groups[0])
    parts = exchange(value, groups)
    return jnp.sum(parts.reshape(n, value.shape[0] // n, value.shape[1]), axis=0)


def replicate(value, n):
    return jnp.broadcast_to(value[None], (n,) + value.shape).reshape(n * value.shape[0], value.shape[1])


def all_sum(value, groups):
    return scatter_sum(replicate(value, len(groups[0])), groups)


def collect(value, groups):
    return exchange(replicate(value, len(groups[0])), groups)


def all_reduce(kept, sent):
    value = kept + swap(sent)
    value = scatter_sum(value, PLANES)
    value = all_sum(value, LINES)
    return collect(value, PLANES)


def dot(left, right, dims):
    return lax.dot_general(left, right, (dims, ((), ())), precision=lax.Precision.HIGHEST, preferred_element_type=jnp.float32)


def up(count, to):
    return -(-count // to) * to


def params():
    return pltpu.CompilerParams(vmem_limit_bytes=VMEM_LIMIT)


def core():
    return lax.rem(lax.axis_index("group"), 2)


def in_order(mine, other):
    first = core() == 0
    return jnp.where(first, mine, other), jnp.where(first, other, mine)


def stage_kernel(owners, offsets, points, kept, sent):
    here = lax.axis_index(AXES)
    features, width = points.shape
    for step, out in ((core(), kept), (1 - core(), sent)):

        @pl.when(owners[step] == here)
        def _():
            turned = pltpu.roll(points[...], lax.rem(width - offsets[step], width), axis=1)
            out[:features, :] = turned[:, :LANES]
            out[features : 2 * features, :] = turned[:, LANES : 2 * LANES]
            out[2 * features :, :] = jnp.zeros((out.shape[0] - 2 * features, LANES), jnp.float32)

        @pl.when(owners[step] != here)
        def _():
            out[...] = jnp.zeros(out.shape, jnp.float32)


def stage(owners, offsets, points):
    half = jax.ShapeDtypeStruct((up(2 * points.shape[0], 128), LANES), jnp.float32)
    return pl.pallas_call(
        stage_kernel,
        out_shape=(half, half),
        in_specs=[SMEM, SMEM, VMEM],
        out_specs=(VMEM, VMEM),
        name="stage",
        compiler_params=params(),
    )(owners, offsets, points)


def kernel_values(left, right):
    features = left.shape[0]
    down = jnp.broadcast_to(jnp.sum(left * left, axis=0, keepdims=True), (8, left.shape[1])).T[:, :1]
    along = jnp.sum(right * right, axis=0, keepdims=True)
    return jnp.exp((2.0 * dot(left, right, ((0,), (0,))) - down - along) * (1.0 / features))


def tiles_kernel(mine, other, points, residual, tiles, kept, sent):
    features, classes = points.shape[0], residual.shape[0]
    rows = up(classes, 8)
    pieces = [half[i * features : (i + 1) * features, :] for half in in_order(mine[...], other[...]) for i in range(2)]
    tiles[...] = kernel_values(jnp.concatenate(pieces, axis=1), points[...])
    grads = dot(residual[...], tiles[...], ((1,), (1,)))
    overlap = dot(tiles[:BLOCK, :], tiles[BLOCK:, :], ((1,), (1,)))
    gap = jnp.zeros((rows - classes, LANES), jnp.float32)
    halves = []
    for step in range(2):
        left, right = (grads[:, (2 * step + i) * LANES : (2 * step + i + 1) * LANES] for i in range(2))
        end = jnp.zeros((kept.shape[0] - 2 * rows - BLOCK, LANES), jnp.float32)
        halves.append((left, right, overlap[:, step * LANES : (step + 1) * LANES], end))
    for out, own in ((kept, 0), (sent, 1)):
        left, right, products, end = (in_order(a, b)[own] for a, b in zip(*halves))
        out[:classes, :] = left
        out[classes:rows, :] = gap
        out[rows : rows + classes, :] = right
        out[rows + classes : 2 * rows, :] = gap
        out[2 * rows : 2 * rows + BLOCK, :] = products
        out[2 * rows + BLOCK :, :] = end


def make_tiles(mine, other, points, residual):
    width, rows = points.shape[1], up(residual.shape[0], 8)
    half = jax.ShapeDtypeStruct((up(2 * rows + BLOCK, 128), LANES), jnp.float32)
    return pl.pallas_call(
        tiles_kernel,
        out_shape=(jax.ShapeDtypeStruct((2 * BLOCK, width), jnp.float32), half, half),
        in_specs=[VMEM] * 4,
        out_specs=(VMEM,) * 3,
        name="tiles",
        compiler_params=params(),
    )(mine, other, points, residual)


def gram_kernel(features, mine, gram):
    block = jnp.concatenate([mine[i * features : (i + 1) * features, :] for i in range(2)], axis=1)
    diagonal = lax.broadcasted_iota(jnp.int32, gram.shape, 0) == lax.broadcasted_iota(jnp.int32, gram.shape, 1)
    gram[...] = kernel_values(block, block) + jnp.where(diagonal, ridge, 0.0)


def make_gram(mine, features):
    return pl.pallas_call(
        functools.partial(gram_kernel, features),
        out_shape=jax.ShapeDtypeStruct((BLOCK, BLOCK), jnp.float32),
        in_specs=[VMEM],
        out_specs=VMEM,
        name="gram",
        compiler_params=params(),
        cost_estimate=pl.CostEstimate(flops=SWEEP_FLOPS // 4, bytes_accessed=1 << 20, transcendentals=0),
    )(mine)


def inverse_2(a, b, d):
    r = 1.0 / (a * d - b * b)
    return d * r, -b * r, a * r


def inverse_4(v):
    pair = range(2)
    x, y, z = inverse_2(v[0][0], v[0][1], v[1][1])
    corner = [[x, y], [y, z]]
    right = [[v[i][2 + j] for j in pair] for i in pair]
    u = [[corner[i][0] * right[0][j] + corner[i][1] * right[1][j] for j in pair] for i in pair]
    rest = [[v[2 + i][2 + j] - (right[0][i] * u[0][j] + right[1][i] * u[1][j]) for j in pair] for i in pair]
    e, f, g = inverse_2(rest[0][0], rest[0][1], rest[1][1])
    last = [[e, f], [f, g]]
    w = [[u[i][0] * last[0][j] + u[i][1] * last[1][j] for j in pair] for i in pair]
    first = [[corner[i][j] + w[i][0] * u[j][0] + w[i][1] * u[j][1] for j in pair] for i in pair]
    return [
        [first[0][0], first[0][1], -w[0][0], -w[0][1]],
        [first[0][1], first[1][1], -w[1][0], -w[1][1]],
        [-w[0][0], -w[1][0], e, f],
        [-w[0][1], -w[1][1], f, g],
    ]


def negative_inverse(p):
    n = p.shape[0]
    down = lax.broadcasted_iota(jnp.int32, (n, n), 0)
    along = lax.broadcasted_iota(jnp.int32, (n, n), 1)
    four = range(4)
    for j in range(0, n, 4):
        cols = [jnp.broadcast_to(p[:, j + i : j + i + 1], (n, n)) for i in four]
        rows = [p[j + i : j + i + 1, :] for i in four]
        w = inverse_4([[cols[k][j + i : j + i + 1, :] for k in four] for i in four])
        past = (along[:1] >= j) & (along[:1] < j + 4)
        rows = [jnp.where(past, 0.0, row) for row in rows]
        scaled = [sum(w[i][k] * rows[k] for k in four) for i in four]
        for i in four:
            p = p - cols[i] * scaled[i]
        for k in four:
            fresh = sum(cols[i] * w[i][k] for i in four)
            p = jnp.where(along == j + k, fresh, p)
        for i in four:
            row = scaled[i]
            for k in four:
                row = jnp.where(along[:1] == j + k, -w[i][k], row)
            p = jnp.where(down == j + i, row, p)
    return p


def sweep_kernel(first, last, size, source, out):
    n = out.shape[1]
    for at in range(first, last, size):
        along = lax.broadcasted_iota(jnp.int32, (size, n), 1)
        past = (along >= at) & (along < at + size)
        rows = source[at : at + size, :]
        pivot = negative_inverse(rows[:, at : at + size])
        panel = jnp.where(past, 0.0, rows)
        scaled = dot(pivot, panel, ((1,), (0,)))
        wide = jnp.pad(pivot, ((0, 0), (at, n - at - size)))
        fresh = jnp.where(past, wide, -scaled)
        out[...] = source[...] + dot(panel, scaled, ((0,), (0,)))
        out[at : at + size, :] = fresh
        out[:, at : at + size] = fresh.T
        source = out


def sweep(gram, first, last, size=64):
    return pl.pallas_call(
        functools.partial(sweep_kernel, first, last, size),
        out_shape=jax.ShapeDtypeStruct(gram.shape, gram.dtype),
        in_specs=[VMEM],
        out_specs=VMEM,
        name="sweep",
        compiler_params=params(),
        cost_estimate=pl.CostEstimate(flops=SWEEP_FLOPS * (last - first) // 64, bytes_accessed=1 << 20, transcendentals=0),
    )(gram)


def finish_kernel(
    owners, offsets, my_sums, other_sums, my_inverse, other_inverse, tiles, residual, coeffs, new_residual, new_coeffs
):
    here = lax.axis_index(AXES)
    classes, width = residual.shape
    rows = up(classes, 8)
    sums = in_order(my_sums[...], other_sums[...])
    inverses = in_order(my_inverse[...], other_inverse[...])
    grads = [jnp.concatenate([half[:rows, :], half[rows : 2 * rows, :]], axis=1) for half in sums]
    overlap = jnp.concatenate([half[2 * rows : 2 * rows + BLOCK, :] for half in sums], axis=1)

    def direction(grad, inverse):
        scale = step_norm / jnp.sqrt(jnp.sum(grad * grad) * (1.0 / (classes * BLOCK)) + 1e-06)
        return dot(grad, inverse, ((1,), (0,))) * -scale

    delta0 = direction(grads[0], inverses[0])
    delta1 = direction(grads[1] - dot(delta0, overlap, ((1,), (0,))), inverses[1])
    deltas = [delta[:classes] for delta in (delta0, delta1)]
    new_residual[...] = residual[...] - dot(jnp.concatenate(deltas, axis=1), tiles[...], ((1,), (0,)))
    new_coeffs[...] = coeffs[...]
    for step in range(2):

        @pl.when(owners[step] == here)
        def _():
            wide = jnp.concatenate([deltas[step], jnp.zeros((classes, width - BLOCK), jnp.float32)], axis=1)
            new_coeffs[...] = new_coeffs[...] + pltpu.roll(wide, offsets[step], axis=1)


def finish(owners, offsets, *arrays):
    residual, coeffs = arrays[-2:]
    return pl.pallas_call(
        finish_kernel,
        out_shape=(jax.ShapeDtypeStruct(residual.shape, jnp.float32), jax.ShapeDtypeStruct(coeffs.shape, jnp.float32)),
        in_specs=[SMEM, SMEM] + [VMEM] * 7,
        out_specs=(VMEM, VMEM),
        name="finish",
        compiler_params=params(),
    )(owners, offsets, *arrays)


def body(points, residual, coeffs, owners, offsets):
    mine = all_reduce(*stage(owners, offsets, points))
    tiles, kept, sent = make_tiles(mine, swap(mine), points, residual)
    inverse = make_gram(mine, points.shape[0])
    for at in range(0, BLOCK, 64):
        inverse = sweep(inverse, at, at + 64)
    sums = all_reduce(kept, sent)
    return finish(owners, offsets, sums, swap(sums), inverse, swap(inverse), tiles, residual, coeffs)


def solution(mesh):
    split = P(None, AXES)
    return jax.shard_map(
        body,
        mesh=mesh,
        in_specs=(split, split, split, P(), P()),
        out_specs=(split, split),
        check_vma=False,
    )
```

```python
import functools
import itertools

import jax
import jax.numpy as jnp
from jax import lax
from jax.experimental import pallas as pl
from jax.experimental.pallas import tpu as pltpu
from jax.sharding import PartitionSpec as P

BLOCK = 256
LANES = 128
AXES = ("group", "dev")

VMEM_LIMIT = 24 << 20
SWEEP_FLOPS = 4_000_000_000

ridge = 2.0
step_norm = 1.5

VMEM = pl.BlockSpec(memory_space=pltpu.VMEM)
SMEM = pl.BlockSpec(memory_space=pltpu.SMEM)


def rings():
    ys, cores, zs, xs = range(4), range(2), range(8), range(4)
    at = lambda y, c, z, x: (y * 2 + c) * 32 + z * 4 + x
    turn = lambda seq, c: [(i + 2 * c) % 4 for i in seq]
    planes = [
        [at(y, c, z, x) for y, x in itertools.product(turn(ys, c), turn(xs, c))] for c, z in itertools.product(cores, zs)
    ]
    lines = [[at(y, c, z, x) for z in (0, 4, 2, 6, 1, 5, 3, 7)] for y, c, x in itertools.product(ys, cores, xs)]
    partners = [(at(y, c, z, x), at(y, 1 - c, z, x)) for y, c, z, x in itertools.product(ys, cores, zs, xs)]
    return planes, lines, partners


PLANES, LINES, PARTNERS = rings()


def swap(value):
    return lax.ppermute(value, AXES, PARTNERS)


def exchange(value, groups):
    return lax.all_to_all(value, AXES, 0, 0, tiled=True, axis_index_groups=groups)


def scatter_sum(value, groups):
    n = len(groups[0])
    parts = exchange(value, groups)
    return jnp.sum(parts.reshape(n, value.shape[0] // n, value.shape[1]), axis=0)


def replicate(value, n):
    return jnp.broadcast_to(value[None], (n,) + value.shape).reshape(n * value.shape[0], value.shape[1])


def all_sum(value, groups):
    return scatter_sum(replicate(value, len(groups[0])), groups)


def collect(value, groups):
    return exchange(replicate(value, len(groups[0])), groups)


def all_reduce(kept, sent, beside=None):
    first, second, third = (lambda carry: carry,) * 3 if beside is None else beside
    value = kept + swap(sent)
    value, carry = lax.optimization_barrier((scatter_sum(value, PLANES), first(())))
    value, carry = lax.optimization_barrier((all_sum(value, LINES), second(carry)))
    return lax.optimization_barrier((collect(value, PLANES), third(carry)))


def dot(left, right, dims):
    return lax.dot_general(left, right, (dims, ((), ())), precision=lax.Precision.HIGHEST, preferred_element_type=jnp.float32)


def up(count, to):
    return -(-count // to) * to


def params():
    return pltpu.CompilerParams(vmem_limit_bytes=VMEM_LIMIT)


def core():
    return lax.rem(lax.axis_index("group"), 2)


def in_order(mine, other):
    first = core() == 0
    return jnp.where(first, mine, other), jnp.where(first, other, mine)


def stage_kernel(places, points, kept, sent):
    here = lax.axis_index(AXES)
    features, width = points.shape
    for step, out in ((core(), kept), (1 - core(), sent)):

        @pl.when(places[0, step] == here)
        def _():
            turned = pltpu.roll(points[...], lax.rem(width - places[1, step], width), axis=1)
            out[:features, :] = turned[:, :LANES]
            out[features : 2 * features, :] = turned[:, LANES : 2 * LANES]
            out[2 * features :, :] = jnp.zeros((out.shape[0] - 2 * features, LANES), jnp.float32)

        @pl.when(places[0, step] != here)
        def _():
            out[...] = jnp.zeros(out.shape, jnp.float32)


def stage(places, points):
    half = jax.ShapeDtypeStruct((up(2 * points.shape[0], 128), LANES), jnp.float32)
    return pl.pallas_call(
        stage_kernel,
        out_shape=(half, half),
        in_specs=[SMEM, VMEM],
        out_specs=(VMEM, VMEM),
        name="stage",
        compiler_params=params(),
    )(places, points)


def kernel_values(left, right):
    features = left.shape[0]
    down = jnp.broadcast_to(jnp.sum(left * left, axis=0, keepdims=True), (8, left.shape[1])).T[:, :1]
    along = jnp.sum(right * right, axis=0, keepdims=True)
    return jnp.exp((2.0 * dot(left, right, ((0,), (0,))) - down - along) * (1.0 / features))


def block_of(pieces, features):
    return jnp.concatenate([pieces[i * features : (i + 1) * features, :] for i in range(2)], axis=1)


def tile_kernel(mine, points, residual, tile, grad):
    tile[...] = kernel_values(block_of(mine, points.shape[0]), points[...])
    grad[...] = dot(residual[...], tile[...], ((1,), (1,)))


def make_tile(mine, points, residual):
    return pl.pallas_call(
        tile_kernel,
        out_shape=(
            jax.ShapeDtypeStruct((BLOCK, points.shape[1]), jnp.float32),
            jax.ShapeDtypeStruct((residual.shape[0], BLOCK), jnp.float32),
        ),
        in_specs=[VMEM] * 3,
        out_specs=(VMEM, VMEM),
        name="tile",
        compiler_params=params(),
        cost_estimate=pl.CostEstimate(flops=SWEEP_FLOPS // 4, bytes_accessed=1 << 20, transcendentals=0),
    )(mine, points, residual)


def products_kernel(my_tile, my_grad, other, points, residual, other_tile, kept, sent):
    classes = residual.shape[0]
    rows = up(classes, 8)
    other_tile[...] = kernel_values(block_of(other, points.shape[0]), points[...])
    gap = jnp.zeros((rows - classes, LANES), jnp.float32)
    end = jnp.zeros((kept.shape[0] - 2 * rows - BLOCK, LANES), jnp.float32)
    overlap = dot(*in_order(my_tile[...], other_tile[...]), ((1,), (1,)))
    products = in_order(overlap[:, :LANES], overlap[:, LANES:])
    grads = (my_grad[...], dot(residual[...], other_tile[...], ((1,), (1,))))
    for i, (out, grad) in enumerate(zip((kept, sent), grads)):
        out[:classes, :] = grad[:, :LANES]
        out[classes:rows, :] = gap
        out[rows : rows + classes, :] = grad[:, LANES:]
        out[rows + classes : 2 * rows, :] = gap
        out[2 * rows : 2 * rows + BLOCK, :] = products[i]
        out[2 * rows + BLOCK :, :] = end


def make_products(my_tile, my_grad, other, points, residual):
    half = jax.ShapeDtypeStruct((up(2 * up(residual.shape[0], 8) + BLOCK, 128), LANES), jnp.float32)
    return pl.pallas_call(
        products_kernel,
        out_shape=(jax.ShapeDtypeStruct(my_tile.shape, jnp.float32), half, half),
        in_specs=[VMEM] * 5,
        out_specs=(VMEM,) * 3,
        name="products",
        compiler_params=params(),
    )(my_tile, my_grad, other, points, residual)


def gram_kernel(features, mine, gram):
    block = block_of(mine, features)
    diagonal = lax.broadcasted_iota(jnp.int32, gram.shape, 0) == lax.broadcasted_iota(jnp.int32, gram.shape, 1)
    gram[...] = kernel_values(block, block) + jnp.where(diagonal, ridge, 0.0)


def make_gram(mine, features):
    return pl.pallas_call(
        functools.partial(gram_kernel, features),
        out_shape=jax.ShapeDtypeStruct((BLOCK, BLOCK), jnp.float32),
        in_specs=[VMEM],
        out_specs=VMEM,
        name="gram",
        compiler_params=params(),
        cost_estimate=pl.CostEstimate(flops=SWEEP_FLOPS // 4, bytes_accessed=1 << 20, transcendentals=0),
    )(mine)


def inverse_2(a, b, d):
    r = 1.0 / (a * d - b * b)
    return d * r, -b * r, a * r


def inverse_4(v):
    pair = range(2)
    x, y, z = inverse_2(v[0][0], v[0][1], v[1][1])
    corner = [[x, y], [y, z]]
    right = [[v[i][2 + j] for j in pair] for i in pair]
    u = [[corner[i][0] * right[0][j] + corner[i][1] * right[1][j] for j in pair] for i in pair]
    rest = [[v[2 + i][2 + j] - (right[0][i] * u[0][j] + right[1][i] * u[1][j]) for j in pair] for i in pair]
    e, f, g = inverse_2(rest[0][0], rest[0][1], rest[1][1])
    last = [[e, f], [f, g]]
    w = [[u[i][0] * last[0][j] + u[i][1] * last[1][j] for j in pair] for i in pair]
    first = [[corner[i][j] + w[i][0] * u[j][0] + w[i][1] * u[j][1] for j in pair] for i in pair]
    return [
        [first[0][0], first[0][1], -w[0][0], -w[0][1]],
        [first[0][1], first[1][1], -w[1][0], -w[1][1]],
        [-w[0][0], -w[1][0], e, f],
        [-w[0][1], -w[1][1], f, g],
    ]


def negative_inverse(p):
    n = p.shape[0]
    down = lax.broadcasted_iota(jnp.int32, (n, n), 0)
    along = lax.broadcasted_iota(jnp.int32, (n, n), 1)
    four = range(4)
    for j in range(0, n, 4):
        cols = [jnp.broadcast_to(p[:, j + i : j + i + 1], (n, n)) for i in four]
        rows = [p[j + i : j + i + 1, :] for i in four]
        w = inverse_4([[cols[k][j + i : j + i + 1, :] for k in four] for i in four])
        past = (along[:1] >= j) & (along[:1] < j + 4)
        rows = [jnp.where(past, 0.0, row) for row in rows]
        scaled = [sum(w[i][k] * rows[k] for k in four) for i in four]
        for i in four:
            p = p - cols[i] * scaled[i]
        for k in four:
            fresh = sum(cols[i] * w[i][k] for i in four)
            p = jnp.where(along == j + k, fresh, p)
        for i in four:
            row = scaled[i]
            for k in four:
                row = jnp.where(along[:1] == j + k, -w[i][k], row)
            p = jnp.where(down == j + i, row, p)
    return p


def sweep_kernel(first, last, size, source, out):
    n = out.shape[1]
    for at in range(first, last, size):
        along = lax.broadcasted_iota(jnp.int32, (size, n), 1)
        past = (along >= at) & (along < at + size)
        rows = source[at : at + size, :]
        pivot = negative_inverse(rows[:, at : at + size])
        panel = jnp.where(past, 0.0, rows)
        scaled = dot(pivot, panel, ((1,), (0,)))
        wide = jnp.pad(pivot, ((0, 0), (at, n - at - size)))
        fresh = jnp.where(past, wide, -scaled)
        out[...] = source[...] + dot(panel, scaled, ((0,), (0,)))
        out[at : at + size, :] = fresh
        out[:, at : at + size] = fresh.T
        source = out


def sweep(gram, first, last, size=64):
    return pl.pallas_call(
        functools.partial(sweep_kernel, first, last, size),
        out_shape=jax.ShapeDtypeStruct(gram.shape, gram.dtype),
        in_specs=[VMEM],
        out_specs=VMEM,
        name="sweep",
        compiler_params=params(),
        cost_estimate=pl.CostEstimate(flops=SWEEP_FLOPS * (last - first) // 64, bytes_accessed=1 << 20, transcendentals=0),
    )(gram)


def finish_kernel(
    places, my_sums, other_sums, my_inverse, other_inverse, my_tile, other_tile, residual, coeffs, new_residual, new_coeffs
):
    here = lax.axis_index(AXES)
    classes, width = residual.shape
    rows = up(classes, 8)
    sums = in_order(my_sums[...], other_sums[...])
    inverses = in_order(my_inverse[...], other_inverse[...])
    grads = [jnp.concatenate([half[:rows, :], half[rows : 2 * rows, :]], axis=1) for half in sums]
    overlap = jnp.concatenate([half[2 * rows : 2 * rows + BLOCK, :] for half in sums], axis=1)

    def direction(grad, inverse):
        scale = step_norm / jnp.sqrt(jnp.sum(grad * grad) * (1.0 / (classes * BLOCK)) + 1e-06)
        return dot(grad, inverse, ((1,), (0,))) * -scale

    delta0 = direction(grads[0], inverses[0])
    delta1 = direction(grads[1] - dot(delta0, overlap, ((1,), (0,))), inverses[1])
    deltas = [delta[:classes] for delta in (delta0, delta1)]
    tiles = in_order(my_tile[...], other_tile[...])
    after0 = residual[...] - dot(deltas[0], tiles[0], ((1,), (0,)))
    new_residual[...] = after0 - dot(deltas[1], tiles[1], ((1,), (0,)))
    new_coeffs[...] = coeffs[...]
    for step in range(2):

        @pl.when(places[0, step] == here)
        def _():
            wide = jnp.concatenate([deltas[step], jnp.zeros((classes, width - BLOCK), jnp.float32)], axis=1)
            new_coeffs[...] = new_coeffs[...] + pltpu.roll(wide, places[1, step], axis=1)


def finish(places, *arrays):
    residual, coeffs = arrays[-2:]
    return pl.pallas_call(
        finish_kernel,
        out_shape=(jax.ShapeDtypeStruct(residual.shape, jnp.float32), jax.ShapeDtypeStruct(coeffs.shape, jnp.float32)),
        in_specs=[SMEM] + [VMEM] * 8,
        out_specs=(VMEM, VMEM),
        name="finish",
        compiler_params=params(),
    )(places, *arrays)


def body(points, residual, coeffs, owners, offsets):
    places = jnp.stack([owners, offsets])
    mine, _ = all_reduce(*stage(places, points))
    other, (my_tile, my_grad) = lax.optimization_barrier((swap(mine), make_tile(mine, points, residual)))
    other_tile, kept, sent = make_products(my_tile, my_grad, other, points, residual)
    gram = make_gram(mine, points.shape[0])

    def last(gram):
        inverse = sweep(gram, 192, 256)
        return inverse, swap(inverse)

    sums, inverses = all_reduce(kept, sent, (lambda _: sweep(gram, 0, 128), lambda m: sweep(m, 128, 192), last))
    return finish(places, sums, swap(sums), *inverses, my_tile, other_tile, residual, coeffs)


def solution(mesh):
    split = P(None, AXES)
    return jax.shard_map(
        body,
        mesh=mesh,
        in_specs=(split, split, split, P(), P()),
        out_specs=(split, split),
        check_vma=False,
    )
```

```python
import functools
import itertools

import jax
import jax.numpy as jnp
from jax import lax
from jax.experimental import pallas as pl
from jax.experimental.pallas import tpu as pltpu
from jax.sharding import PartitionSpec as P

BLOCK = 256
LANES = 128
AXES = ("group", "dev")

VMEM_LIMIT = 24 << 20
SWEEP_FLOPS = 4_000_000_000

ridge = 2.0
step_norm = 1.5

VMEM = pl.BlockSpec(memory_space=pltpu.VMEM)
SMEM = pl.BlockSpec(memory_space=pltpu.SMEM)


def rings():
    ys, cores, zs, xs = range(4), range(2), range(8), range(4)
    at = lambda y, c, z, x: (y * 2 + c) * 32 + z * 4 + x
    planes = [[at(y, c, z, x) for y, x in itertools.product((2, 3, 0, 1), repeat=2)] for c, z in itertools.product(cores, zs)]
    lines = [[at(y, c, z, x) for z in (7, 3, 5, 1, 6, 2, 4, 0)] for y, c, x in itertools.product(ys, cores, xs)]
    partners = [(at(y, c, z, x), at(y, 1 - c, z, x)) for y, c, z, x in itertools.product(ys, cores, zs, xs)]
    return planes, lines, partners


PLANES, LINES, PARTNERS = rings()


def swap(value):
    return lax.ppermute(value, AXES, PARTNERS)


def exchange(value, groups):
    return lax.all_to_all(value, AXES, 0, 0, tiled=True, axis_index_groups=groups)


def scatter_sum(value, groups):
    n = len(groups[0])
    parts = exchange(value, groups)
    return jnp.sum(parts.reshape(n, value.shape[0] // n, value.shape[1]), axis=0)


def replicate(value, n):
    return jnp.broadcast_to(value[None], (n,) + value.shape).reshape(n * value.shape[0], value.shape[1])


def all_sum(value, groups):
    return scatter_sum(replicate(value, len(groups[0])), groups)


def collect(value, groups):
    return exchange(replicate(value, len(groups[0])), groups)


def all_reduce(kept, sent, beside=None):
    first, second, third = (lambda carry: carry,) * 3 if beside is None else beside
    value = kept + swap(sent)
    value, carry = lax.optimization_barrier((scatter_sum(value, PLANES), first(())))
    value, carry = lax.optimization_barrier((all_sum(value, LINES), second(carry)))
    return lax.optimization_barrier((collect(value, PLANES), third(carry)))


def dot(left, right, dims):
    return lax.dot_general(left, right, (dims, ((), ())), precision=lax.Precision.HIGHEST, preferred_element_type=jnp.float32)


def halves(value):
    high = value.astype(jnp.bfloat16)
    return high, (value - high.astype(jnp.float32)).astype(jnp.bfloat16)


def dot_3(left, right, dims):
    (left, left_rest), (right, right_rest) = halves(left), halves(right)
    product = lambda a, b: lax.dot_general(a, b, (dims, ((), ())), preferred_element_type=jnp.float32)
    return product(left, right_rest) + product(left_rest, right) + product(left, right)


def up(count, to):
    return -(-count // to) * to


def params():
    return pltpu.CompilerParams(vmem_limit_bytes=VMEM_LIMIT)


def core():
    return lax.rem(lax.axis_index("group"), 2)


def in_order(mine, other):
    first = core() == 0
    return jnp.where(first, mine, other), jnp.where(first, other, mine)


def stage_kernel(places, points, kept, sent):
    here = lax.axis_index(AXES)
    features, width = points.shape
    for step, out in ((core(), kept), (1 - core(), sent)):

        @pl.when(places[0, step] == here)
        def _():
            turned = pltpu.roll(points[...], lax.rem(width - places[1, step], width), axis=1)
            out[:features, :] = turned[:, :LANES]
            out[features : 2 * features, :] = turned[:, LANES : 2 * LANES]
            out[2 * features :, :] = jnp.zeros((out.shape[0] - 2 * features, LANES), jnp.float32)

        @pl.when(places[0, step] != here)
        def _():
            out[...] = jnp.zeros(out.shape, jnp.float32)


def stage(places, points):
    half = jax.ShapeDtypeStruct((up(2 * points.shape[0], 128), LANES), jnp.float32)
    return pl.pallas_call(
        stage_kernel,
        out_shape=(half, half),
        in_specs=[SMEM, VMEM],
        out_specs=(VMEM, VMEM),
        name="stage",
        compiler_params=params(),
    )(places, points)


def kernel_values(left, right):
    features = left.shape[0]
    down = jnp.broadcast_to(jnp.sum(left * left, axis=0, keepdims=True), (8, left.shape[1])).T[:, :1]
    along = jnp.sum(right * right, axis=0, keepdims=True)
    return jnp.exp((2.0 * dot(left, right, ((0,), (0,))) - down - along) * (1.0 / features))


def block_of(pieces, features):
    return jnp.concatenate([pieces[i * features : (i + 1) * features, :] for i in range(2)], axis=1)


def tile_kernel(mine, points, residual, tile, grad):
    tile[...] = kernel_values(block_of(mine, points.shape[0]), points[...])
    grad[...] = dot_3(residual[...], tile[...], ((1,), (1,)))


def make_tile(mine, points, residual):
    return pl.pallas_call(
        tile_kernel,
        out_shape=(
            jax.ShapeDtypeStruct((BLOCK, points.shape[1]), jnp.float32),
            jax.ShapeDtypeStruct((residual.shape[0], BLOCK), jnp.float32),
        ),
        in_specs=[VMEM] * 3,
        out_specs=(VMEM, VMEM),
        name="tile",
        compiler_params=params(),
        cost_estimate=pl.CostEstimate(flops=SWEEP_FLOPS // 4, bytes_accessed=1 << 20, transcendentals=0),
    )(mine, points, residual)


def products_kernel(my_tile, my_grad, other, points, residual, other_tile, kept, sent):
    classes = residual.shape[0]
    rows = up(classes, 8)
    other_tile[...] = kernel_values(block_of(other, points.shape[0]), points[...])
    gap = jnp.zeros((rows - classes, LANES), jnp.float32)
    end = jnp.zeros((kept.shape[0] - 2 * rows - BLOCK, LANES), jnp.float32)
    overlap = dot_3(*in_order(my_tile[...], other_tile[...]), ((1,), (1,)))
    products = in_order(overlap[:, :LANES], overlap[:, LANES:])
    grads = (my_grad[...], dot_3(residual[...], other_tile[...], ((1,), (1,))))
    for i, (out, grad) in enumerate(zip((kept, sent), grads)):
        out[:classes, :] = grad[:, :LANES]
        out[classes:rows, :] = gap
        out[rows : rows + classes, :] = grad[:, LANES:]
        out[rows + classes : 2 * rows, :] = gap
        out[2 * rows : 2 * rows + BLOCK, :] = products[i]
        out[2 * rows + BLOCK :, :] = end


def make_products(my_tile, my_grad, other, points, residual):
    half = jax.ShapeDtypeStruct((up(2 * up(residual.shape[0], 8) + BLOCK, 128), LANES), jnp.float32)
    return pl.pallas_call(
        products_kernel,
        out_shape=(jax.ShapeDtypeStruct(my_tile.shape, jnp.float32), half, half),
        in_specs=[VMEM] * 5,
        out_specs=(VMEM,) * 3,
        name="products",
        compiler_params=params(),
    )(my_tile, my_grad, other, points, residual)


def gram_kernel(features, mine, gram):
    block = block_of(mine, features)
    diagonal = lax.broadcasted_iota(jnp.int32, gram.shape, 0) == lax.broadcasted_iota(jnp.int32, gram.shape, 1)
    gram[...] = kernel_values(block, block) + jnp.where(diagonal, ridge, 0.0)


def make_gram(mine, features):
    return pl.pallas_call(
        functools.partial(gram_kernel, features),
        out_shape=jax.ShapeDtypeStruct((BLOCK, BLOCK), jnp.float32),
        in_specs=[VMEM],
        out_specs=VMEM,
        name="gram",
        compiler_params=params(),
        cost_estimate=pl.CostEstimate(flops=SWEEP_FLOPS // 4, bytes_accessed=1 << 20, transcendentals=0),
    )(mine)


def inverse_2(a, b, d):
    r = 1.0 / (a * d - b * b)
    return d * r, -b * r, a * r


def inverse_4(v):
    pair = range(2)
    x, y, z = inverse_2(v[0][0], v[0][1], v[1][1])
    corner = [[x, y], [y, z]]
    right = [[v[i][2 + j] for j in pair] for i in pair]
    u = [[corner[i][0] * right[0][j] + corner[i][1] * right[1][j] for j in pair] for i in pair]
    rest = [[v[2 + i][2 + j] - (right[0][i] * u[0][j] + right[1][i] * u[1][j]) for j in pair] for i in pair]
    e, f, g = inverse_2(rest[0][0], rest[0][1], rest[1][1])
    last = [[e, f], [f, g]]
    w = [[u[i][0] * last[0][j] + u[i][1] * last[1][j] for j in pair] for i in pair]
    first = [[corner[i][j] + w[i][0] * u[j][0] + w[i][1] * u[j][1] for j in pair] for i in pair]
    return [
        [first[0][0], first[0][1], -w[0][0], -w[0][1]],
        [first[0][1], first[1][1], -w[1][0], -w[1][1]],
        [-w[0][0], -w[1][0], e, f],
        [-w[0][1], -w[1][1], f, g],
    ]


def negative_inverse(p):
    n = p.shape[0]
    down = lax.broadcasted_iota(jnp.int32, (n, n), 0)
    along = lax.broadcasted_iota(jnp.int32, (n, n), 1)
    four = range(4)
    for j in range(0, n, 4):
        cols = [jnp.broadcast_to(p[:, j + i : j + i + 1], (n, n)) for i in four]
        rows = [p[j + i : j + i + 1, :] for i in four]
        w = inverse_4([[cols[k][j + i : j + i + 1, :] for k in four] for i in four])
        past = (along[:1] >= j) & (along[:1] < j + 4)
        rows = [jnp.where(past, 0.0, row) for row in rows]
        scaled = [sum(w[i][k] * rows[k] for k in four) for i in four]
        for i in four:
            p = p - cols[i] * scaled[i]
        for k in four:
            fresh = sum(cols[i] * w[i][k] for i in four)
            p = jnp.where(along == j + k, fresh, p)
        for i in four:
            row = scaled[i]
            for k in four:
                row = jnp.where(along[:1] == j + k, -w[i][k], row)
            p = jnp.where(down == j + i, row, p)
    return p


def sweep_kernel(first, last, size, source, out):
    n = out.shape[1]
    for at in range(first, last, size):
        along = lax.broadcasted_iota(jnp.int32, (size, n), 1)
        past = (along >= at) & (along < at + size)
        rows = source[at : at + size, :]
        pivot = negative_inverse(rows[:, at : at + size])
        panel = jnp.where(past, 0.0, rows)
        scaled = dot(pivot, panel, ((1,), (0,)))
        wide = jnp.pad(pivot, ((0, 0), (at, n - at - size)))
        fresh = jnp.where(past, wide, -scaled)
        out[...] = source[...] + dot(panel, scaled, ((0,), (0,)))
        out[at : at + size, :] = fresh
        out[:, at : at + size] = fresh.T
        source = out


def sweep(gram, first, last, size=64):
    return pl.pallas_call(
        functools.partial(sweep_kernel, first, last, size),
        out_shape=jax.ShapeDtypeStruct(gram.shape, gram.dtype),
        in_specs=[VMEM],
        out_specs=VMEM,
        name="sweep",
        compiler_params=params(),
        cost_estimate=pl.CostEstimate(flops=SWEEP_FLOPS * (last - first) // 64, bytes_accessed=1 << 20, transcendentals=0),
    )(gram)


def finish_kernel(
    places, my_sums, other_sums, my_inverse, other_inverse, my_tile, other_tile, residual, coeffs, new_residual, new_coeffs
):
    here = lax.axis_index(AXES)
    classes, width = residual.shape
    rows = up(classes, 8)
    sums = in_order(my_sums[...], other_sums[...])
    inverses = in_order(my_inverse[...], other_inverse[...])
    grads = [jnp.concatenate([half[:rows, :], half[rows : 2 * rows, :]], axis=1) for half in sums]
    overlap = jnp.concatenate([half[2 * rows : 2 * rows + BLOCK, :] for half in sums], axis=1)

    def direction(grad, inverse):
        scale = step_norm / jnp.sqrt(jnp.sum(grad * grad) * (1.0 / (classes * BLOCK)) + 1e-06)
        return dot_3(grad, inverse, ((1,), (0,))) * -scale

    delta0 = direction(grads[0], inverses[0])
    delta1 = direction(grads[1] - dot_3(delta0, overlap, ((1,), (0,))), inverses[1])
    deltas = [delta[:classes] for delta in (delta0, delta1)]
    tiles = in_order(my_tile[...], other_tile[...])
    after0 = residual[...] - dot_3(deltas[0], tiles[0], ((1,), (0,)))
    new_residual[...] = after0 - dot_3(deltas[1], tiles[1], ((1,), (0,)))
    new_coeffs[...] = coeffs[...]
    for step in range(2):

        @pl.when(places[0, step] == here)
        def _():
            wide = jnp.concatenate([deltas[step], jnp.zeros((classes, width - BLOCK), jnp.float32)], axis=1)
            new_coeffs[...] = new_coeffs[...] + pltpu.roll(wide, places[1, step], axis=1)


def finish(places, *arrays):
    residual, coeffs = arrays[-2:]
    return pl.pallas_call(
        finish_kernel,
        out_shape=(jax.ShapeDtypeStruct(residual.shape, jnp.float32), jax.ShapeDtypeStruct(coeffs.shape, jnp.float32)),
        in_specs=[SMEM] + [VMEM] * 8,
        out_specs=(VMEM, VMEM),
        name="finish",
        compiler_params=params(),
    )(places, *arrays)


def body(points, residual, coeffs, owners, offsets):
    places = jnp.stack([owners, offsets])
    mine, _ = all_reduce(*stage(places, points))
    other, (my_tile, my_grad) = lax.optimization_barrier((swap(mine), make_tile(mine, points, residual)))
    other_tile, kept, sent = make_products(my_tile, my_grad, other, points, residual)
    gram = make_gram(mine, points.shape[0])

    def last(gram):
        inverse = sweep(gram, 192, 256)
        return inverse, swap(inverse)

    sums, inverses = all_reduce(kept, sent, (lambda _: sweep(gram, 0, 128), lambda m: sweep(m, 128, 192), last))
    return finish(places, sums, swap(sums), *inverses, my_tile, other_tile, residual, coeffs)


def solution(mesh):
    split = P(None, AXES)
    return jax.shard_map(
        body,
        mesh=mesh,
        in_specs=(split, split, split, P(), P()),
        out_specs=(split, split),
        check_vma=False,
    )
```

```python
import functools
import itertools

import jax
import jax.numpy as jnp
from jax import lax
from jax.experimental import pallas as pl
from jax.experimental.pallas import tpu as pltpu
from jax.sharding import PartitionSpec as P

BLOCK = 256
LANES = 128
AXES = ("group", "dev")

VMEM_LIMIT = 24 << 20
SWEEP_FLOPS = 4_000_000_000

ridge = 2.0
step_norm = 1.5

VMEM = pl.BlockSpec(memory_space=pltpu.VMEM)
SMEM = pl.BlockSpec(memory_space=pltpu.SMEM)


def rings():
    ys, cores, zs, xs = range(4), range(2), range(8), range(4)
    at = lambda y, c, z, x: (y * 2 + c) * 32 + z * 4 + x
    planes = [[at(y, c, z, x) for y, x in itertools.product((2, 3, 0, 1), repeat=2)] for c, z in itertools.product(cores, zs)]
    lines = [[at(y, c, z, x) for z in (7, 3, 5, 1, 6, 2, 4, 0)] for y, c, x in itertools.product(ys, cores, xs)]
    partners = [(at(y, c, z, x), at(y, 1 - c, z, x)) for y, c, z, x in itertools.product(ys, cores, zs, xs)]
    return planes, lines, partners


PLANES, LINES, PARTNERS = rings()


def swap(value):
    return lax.ppermute(value, AXES, PARTNERS)


def exchange(value, groups):
    return lax.all_to_all(value, AXES, 0, 0, tiled=True, axis_index_groups=groups)


def scatter_sum(value, groups):
    n = len(groups[0])
    parts = exchange(value, groups)
    return jnp.sum(parts.reshape(n, value.shape[0] // n, value.shape[1]), axis=0)


def replicate(value, n):
    return jnp.broadcast_to(value[None], (n,) + value.shape).reshape(n * value.shape[0], value.shape[1])


def all_sum(value, groups):
    return scatter_sum(replicate(value, len(groups[0])), groups)


def collect(value, groups):
    return exchange(replicate(value, len(groups[0])), groups)


def all_reduce(kept, sent, beside=None):
    first, second, third = (lambda carry: carry,) * 3 if beside is None else beside
    value = kept + swap(sent)
    value, carry = lax.optimization_barrier((scatter_sum(value, PLANES), first(())))
    value, carry = lax.optimization_barrier((all_sum(value, LINES), second(carry)))
    return lax.optimization_barrier((collect(value, PLANES), third(carry)))


def dot(left, right, dims):
    return lax.dot_general(left, right, (dims, ((), ())), precision=lax.Precision.HIGHEST, preferred_element_type=jnp.float32)


def halves(value):
    high = value.astype(jnp.bfloat16)
    return high, (value - high.astype(jnp.float32)).astype(jnp.bfloat16)


def dot_3(left, right, dims):
    (left, left_rest), (right, right_rest) = halves(left), halves(right)
    product = lambda a, b: lax.dot_general(a, b, (dims, ((), ())), preferred_element_type=jnp.float32)
    return product(left, right_rest) + product(left_rest, right) + product(left, right)


def up(count, to):
    return -(-count // to) * to


def params():
    return pltpu.CompilerParams(vmem_limit_bytes=VMEM_LIMIT)


def core():
    return lax.rem(lax.axis_index("group"), 2)


def in_order(mine, other):
    first = core() == 0
    return jnp.where(first, mine, other), jnp.where(first, other, mine)


def stage_kernel(places, points, kept, sent):
    here = lax.axis_index(AXES)
    features, width = points.shape
    for step, out in ((core(), kept), (1 - core(), sent)):

        @pl.when(places[0, step] == here)
        def _():
            turned = pltpu.roll(points[...], lax.rem(width - places[1, step], width), axis=1)
            out[:features, :] = turned[:, :LANES]
            out[features : 2 * features, :] = turned[:, LANES : 2 * LANES]
            out[2 * features :, :] = jnp.zeros((out.shape[0] - 2 * features, LANES), jnp.float32)

        @pl.when(places[0, step] != here)
        def _():
            out[...] = jnp.zeros(out.shape, jnp.float32)


def stage(places, points):
    half = jax.ShapeDtypeStruct((up(2 * points.shape[0], 128), LANES), jnp.float32)
    return pl.pallas_call(
        stage_kernel,
        out_shape=(half, half),
        in_specs=[SMEM, VMEM],
        out_specs=(VMEM, VMEM),
        name="stage",
        compiler_params=params(),
    )(places, points)


def kernel_values(left, right):
    features = left.shape[0]
    down = jnp.broadcast_to(jnp.sum(left * left, axis=0, keepdims=True), (8, left.shape[1])).T[:, :1]
    along = jnp.sum(right * right, axis=0, keepdims=True)
    return jnp.exp((2.0 * dot(left, right, ((0,), (0,))) - down - along) * (1.0 / features))


def block_of(pieces, features):
    return jnp.concatenate([pieces[i * features : (i + 1) * features, :] for i in range(2)], axis=1)


def tile_kernel(mine, points, residual, tile, grad):
    tile[...] = kernel_values(block_of(mine, points.shape[0]), points[...])
    grad[...] = dot_3(residual[...], tile[...], ((1,), (1,)))


def make_tile(mine, points, residual):
    return pl.pallas_call(
        tile_kernel,
        out_shape=(
            jax.ShapeDtypeStruct((BLOCK, points.shape[1]), jnp.float32),
            jax.ShapeDtypeStruct((residual.shape[0], BLOCK), jnp.float32),
        ),
        in_specs=[VMEM] * 3,
        out_specs=(VMEM, VMEM),
        name="tile",
        compiler_params=params(),
        cost_estimate=pl.CostEstimate(flops=SWEEP_FLOPS // 4, bytes_accessed=1 << 20, transcendentals=0),
    )(mine, points, residual)


def products_kernel(my_tile, my_grad, other, points, residual, other_tile, kept, sent):
    classes = residual.shape[0]
    rows = up(classes, 8)
    other_tile[...] = kernel_values(block_of(other, points.shape[0]), points[...])
    gap = jnp.zeros((rows - classes, LANES), jnp.float32)
    end = jnp.zeros((kept.shape[0] - 2 * rows - BLOCK, LANES), jnp.float32)
    overlap = dot_3(*in_order(my_tile[...], other_tile[...]), ((1,), (1,)))
    products = in_order(overlap[:, :LANES], overlap[:, LANES:])
    grads = (my_grad[...], dot_3(residual[...], other_tile[...], ((1,), (1,))))
    for i, (out, grad) in enumerate(zip((kept, sent), grads)):
        out[:classes, :] = grad[:, :LANES]
        out[classes:rows, :] = gap
        out[rows : rows + classes, :] = grad[:, LANES:]
        out[rows + classes : 2 * rows, :] = gap
        out[2 * rows : 2 * rows + BLOCK, :] = products[i]
        out[2 * rows + BLOCK :, :] = end


def make_products(my_tile, my_grad, other, points, residual):
    half = jax.ShapeDtypeStruct((up(2 * up(residual.shape[0], 8) + BLOCK, 128), LANES), jnp.float32)
    return pl.pallas_call(
        products_kernel,
        out_shape=(jax.ShapeDtypeStruct(my_tile.shape, jnp.float32), half, half),
        in_specs=[VMEM] * 5,
        out_specs=(VMEM,) * 3,
        name="products",
        compiler_params=params(),
    )(my_tile, my_grad, other, points, residual)


def gram_kernel(features, mine, gram):
    block = block_of(mine, features)
    diagonal = lax.broadcasted_iota(jnp.int32, gram.shape, 0) == lax.broadcasted_iota(jnp.int32, gram.shape, 1)
    gram[...] = kernel_values(block, block) + jnp.where(diagonal, ridge, 0.0)


def make_gram(mine, features):
    return pl.pallas_call(
        functools.partial(gram_kernel, features),
        out_shape=jax.ShapeDtypeStruct((BLOCK, BLOCK), jnp.float32),
        in_specs=[VMEM],
        out_specs=VMEM,
        name="gram",
        compiler_params=params(),
        cost_estimate=pl.CostEstimate(flops=SWEEP_FLOPS // 4, bytes_accessed=1 << 20, transcendentals=0),
    )(mine)


def inverse_2(a, b, d):
    r = 1.0 / (a * d - b * b)
    return d * r, -b * r, a * r


def inverse_4(v):
    pair = range(2)
    x, y, z = inverse_2(v[0][0], v[0][1], v[1][1])
    corner = [[x, y], [y, z]]
    right = [[v[i][2 + j] for j in pair] for i in pair]
    u = [[corner[i][0] * right[0][j] + corner[i][1] * right[1][j] for j in pair] for i in pair]
    rest = [[v[2 + i][2 + j] - (right[0][i] * u[0][j] + right[1][i] * u[1][j]) for j in pair] for i in pair]
    e, f, g = inverse_2(rest[0][0], rest[0][1], rest[1][1])
    last = [[e, f], [f, g]]
    w = [[u[i][0] * last[0][j] + u[i][1] * last[1][j] for j in pair] for i in pair]
    first = [[corner[i][j] + w[i][0] * u[j][0] + w[i][1] * u[j][1] for j in pair] for i in pair]
    return [
        [first[0][0], first[0][1], -w[0][0], -w[0][1]],
        [first[0][1], first[1][1], -w[1][0], -w[1][1]],
        [-w[0][0], -w[1][0], e, f],
        [-w[0][1], -w[1][1], f, g],
    ]


def negative_inverse(p):
    n = p.shape[0]
    down = lax.broadcasted_iota(jnp.int32, (n, n), 0)
    along = lax.broadcasted_iota(jnp.int32, (n, n), 1)
    four = range(4)
    for j in range(0, n, 4):
        cols = [jnp.broadcast_to(p[:, j + i : j + i + 1], (n, n)) for i in four]
        rows = [p[j + i : j + i + 1, :] for i in four]
        w = inverse_4([[cols[k][j + i : j + i + 1, :] for k in four] for i in four])
        past = (along[:1] >= j) & (along[:1] < j + 4)
        rows = [jnp.where(past, 0.0, row) for row in rows]
        scaled = [sum(w[i][k] * rows[k] for k in four) for i in four]
        for i in four:
            p = p - cols[i] * scaled[i]
        for k in four:
            fresh = sum(cols[i] * w[i][k] for i in four)
            p = jnp.where(along == j + k, fresh, p)
        for i in four:
            row = scaled[i]
            for k in four:
                row = jnp.where(along[:1] == j + k, -w[i][k], row)
            p = jnp.where(down == j + i, row, p)
    return p


def sweep_kernel(spans, source, out):
    n = out.shape[1]
    for at, size in spans:
        along = lax.broadcasted_iota(jnp.int32, (size, n), 1)
        past = (along >= at) & (along < at + size)
        rows = source[at : at + size, :]
        pivot = negative_inverse(rows[:, at : at + size])
        panel = jnp.where(past, 0.0, rows)
        scaled = dot(pivot, panel, ((1,), (0,)))
        wide = jnp.pad(pivot, ((0, 0), (at, n - at - size)))
        fresh = jnp.where(past, wide, -scaled)
        out[...] = source[...] + dot(panel, scaled, ((0,), (0,)))
        out[at : at + size, :] = fresh
        out[:, at : at + size] = fresh.T
        source = out


def sweep(gram, *spans):
    return pl.pallas_call(
        functools.partial(sweep_kernel, spans),
        out_shape=jax.ShapeDtypeStruct(gram.shape, gram.dtype),
        in_specs=[VMEM],
        out_specs=VMEM,
        name="sweep",
        compiler_params=params(),
        cost_estimate=pl.CostEstimate(flops=SWEEP_FLOPS * sum(size for _, size in spans) // 64, bytes_accessed=1 << 20, transcendentals=0),
    )(gram)


def finish_kernel(
    places, my_sums, other_sums, my_inverse, other_inverse, my_tile, other_tile, residual, coeffs, new_residual, new_coeffs
):
    here = lax.axis_index(AXES)
    classes, width = residual.shape
    rows = up(classes, 8)
    sums = in_order(my_sums[...], other_sums[...])
    inverses = in_order(my_inverse[...], other_inverse[...])
    grads = [jnp.concatenate([half[:rows, :], half[rows : 2 * rows, :]], axis=1) for half in sums]
    overlap = jnp.concatenate([half[2 * rows : 2 * rows + BLOCK, :] for half in sums], axis=1)

    def direction(grad, inverse):
        scale = step_norm / jnp.sqrt(jnp.sum(grad * grad) * (1.0 / (classes * BLOCK)) + 1e-06)
        return dot_3(grad, inverse, ((1,), (0,))) * -scale

    delta0 = direction(grads[0], inverses[0])
    delta1 = direction(grads[1] - dot_3(delta0, overlap, ((1,), (0,))), inverses[1])
    deltas = [delta[:classes] for delta in (delta0, delta1)]
    tiles = in_order(my_tile[...], other_tile[...])
    after0 = residual[...] - dot_3(deltas[0], tiles[0], ((1,), (0,)))
    new_residual[...] = after0 - dot_3(deltas[1], tiles[1], ((1,), (0,)))
    new_coeffs[...] = coeffs[...]
    for step in range(2):

        @pl.when(places[0, step] == here)
        def _():
            wide = jnp.concatenate([deltas[step], jnp.zeros((classes, width - BLOCK), jnp.float32)], axis=1)
            new_coeffs[...] = new_coeffs[...] + pltpu.roll(wide, places[1, step], axis=1)


def finish(places, *arrays):
    residual, coeffs = arrays[-2:]
    return pl.pallas_call(
        finish_kernel,
        out_shape=(jax.ShapeDtypeStruct(residual.shape, jnp.float32), jax.ShapeDtypeStruct(coeffs.shape, jnp.float32)),
        in_specs=[SMEM] + [VMEM] * 8,
        out_specs=(VMEM, VMEM),
        name="finish",
        compiler_params=params(),
    )(places, *arrays)


def body(points, residual, coeffs, owners, offsets):
    places = jnp.stack([owners, offsets])
    mine, _ = all_reduce(*stage(places, points))
    other, (my_tile, my_grad) = lax.optimization_barrier((swap(mine), make_tile(mine, points, residual)))
    other_tile, kept, sent = make_products(my_tile, my_grad, other, points, residual)
    gram = make_gram(mine, points.shape[0])

    def last(gram):
        inverse = sweep(gram, (192, 64))
        return inverse, swap(inverse)

    sums, inverses = all_reduce(kept, sent, (lambda _: sweep(gram, (0, 64), (64, 32)), lambda m: sweep(m, (96, 32), (128, 64)), last))
    return finish(places, sums, swap(sums), *inverses, my_tile, other_tile, residual, coeffs)


def solution(mesh):
    split = P(None, AXES)
    return jax.shard_map(
        body,
        mesh=mesh,
        in_specs=(split, split, split, P(), P()),
        out_specs=(split, split),
        check_vma=False,
    )
```

```python
import functools
import itertools

import jax
import jax.numpy as jnp
from jax import lax
from jax.experimental import pallas as pl
from jax.experimental.pallas import tpu as pltpu
from jax.sharding import PartitionSpec as P

BLOCK = 256
LANES = 128
AXES = ("group", "dev")

VMEM_LIMIT = 24 << 20
SWEEP_FLOPS = 4_000_000_000

ridge = 2.0
step_norm = 1.5

VMEM = pl.BlockSpec(memory_space=pltpu.VMEM)
SMEM = pl.BlockSpec(memory_space=pltpu.SMEM)


def rings():
    ys, cores, zs, xs = range(4), range(2), range(8), range(4)
    at = lambda y, c, z, x: (y * 2 + c) * 32 + z * 4 + x
    planes = [[at(y, c, z, x) for y, x in itertools.product((3, 0, 1, 2), repeat=2)] for c, z in itertools.product(cores, zs)]
    lines = [[at(y, c, z, x) for z in (7, 3, 5, 1, 6, 2, 4, 0)] for y, c, x in itertools.product(ys, cores, xs)]
    partners = [(at(y, c, z, x), at(y, 1 - c, z, x)) for y, c, z, x in itertools.product(ys, cores, zs, xs)]
    return planes, lines, partners


PLANES, LINES, PARTNERS = rings()


def swap(value):
    return lax.ppermute(value, AXES, PARTNERS)


def exchange(value, groups):
    return lax.all_to_all(value, AXES, 0, 0, tiled=True, axis_index_groups=groups)


def scatter_sum(value, groups):
    n = len(groups[0])
    parts = exchange(value, groups)
    return jnp.sum(parts.reshape(n, value.shape[0] // n, value.shape[1]), axis=0)


def replicate(value, n):
    return jnp.broadcast_to(value[None], (n,) + value.shape).reshape(n * value.shape[0], value.shape[1])


def all_sum(value, groups):
    return scatter_sum(replicate(value, len(groups[0])), groups)


def collect(value, groups):
    return exchange(replicate(value, len(groups[0])), groups)


def all_reduce(kept, sent, beside=None):
    first, second, third = (lambda carry: carry,) * 3 if beside is None else beside
    value = kept + swap(sent)
    value, carry = lax.optimization_barrier((scatter_sum(value, PLANES), first(())))
    value, carry = lax.optimization_barrier((all_sum(value, LINES), second(carry)))
    return lax.optimization_barrier((collect(value, PLANES), third(carry)))


def dot(left, right, dims):
    return lax.dot_general(left, right, (dims, ((), ())), precision=lax.Precision.HIGHEST, preferred_element_type=jnp.float32)


def halves(value):
    high = value.astype(jnp.bfloat16)
    return high, (value - high.astype(jnp.float32)).astype(jnp.bfloat16)


def dot_3(left, right, dims):
    (left, left_rest), (right, right_rest) = halves(left), halves(right)
    product = lambda a, b: lax.dot_general(a, b, (dims, ((), ())), preferred_element_type=jnp.float32)
    return product(left, right_rest) + product(left_rest, right) + product(left, right)


def up(count, to):
    return -(-count // to) * to


def params():
    return pltpu.CompilerParams(vmem_limit_bytes=VMEM_LIMIT)


def core():
    return lax.rem(lax.axis_index("group"), 2)


def in_order(mine, other):
    first = core() == 0
    return jnp.where(first, mine, other), jnp.where(first, other, mine)


def stage_kernel(places, points, kept, sent):
    here = lax.axis_index(AXES)
    features, width = points.shape
    for step, out in ((core(), kept), (1 - core(), sent)):

        @pl.when(places[0, step] == here)
        def _():
            turned = pltpu.roll(points[...], lax.rem(width - places[1, step], width), axis=1)
            out[:features, :] = turned[:, :LANES]
            out[features : 2 * features, :] = turned[:, LANES : 2 * LANES]
            out[2 * features :, :] = jnp.zeros((out.shape[0] - 2 * features, LANES), jnp.float32)

        @pl.when(places[0, step] != here)
        def _():
            out[...] = jnp.zeros(out.shape, jnp.float32)


def stage(places, points):
    half = jax.ShapeDtypeStruct((up(2 * points.shape[0], 128), LANES), jnp.float32)
    return pl.pallas_call(
        stage_kernel,
        out_shape=(half, half),
        in_specs=[SMEM, VMEM],
        out_specs=(VMEM, VMEM),
        name="stage",
        compiler_params=params(),
    )(places, points)


def kernel_values(left, right):
    features = left.shape[0]
    down = jnp.broadcast_to(jnp.sum(left * left, axis=0, keepdims=True), (8, left.shape[1])).T[:, :1]
    along = jnp.sum(right * right, axis=0, keepdims=True)
    return jnp.exp((2.0 * dot(left, right, ((0,), (0,))) - down - along) * (1.0 / features))


def block_of(pieces, features):
    return jnp.concatenate([pieces[i * features : (i + 1) * features, :] for i in range(2)], axis=1)


def tile_kernel(mine, points, residual, tile, grad):
    tile[...] = kernel_values(block_of(mine, points.shape[0]), points[...])
    grad[...] = dot_3(residual[...], tile[...], ((1,), (1,)))


def make_tile(mine, points, residual):
    return pl.pallas_call(
        tile_kernel,
        out_shape=(
            jax.ShapeDtypeStruct((BLOCK, points.shape[1]), jnp.float32),
            jax.ShapeDtypeStruct((residual.shape[0], BLOCK), jnp.float32),
        ),
        in_specs=[VMEM] * 3,
        out_specs=(VMEM, VMEM),
        name="tile",
        compiler_params=params(),
        cost_estimate=pl.CostEstimate(flops=SWEEP_FLOPS // 4, bytes_accessed=1 << 20, transcendentals=0),
    )(mine, points, residual)


def products_kernel(my_tile, my_grad, other, points, residual, other_tile, kept, sent):
    classes = residual.shape[0]
    rows = up(classes, 8)
    other_tile[...] = kernel_values(block_of(other, points.shape[0]), points[...])
    gap = jnp.zeros((rows - classes, LANES), jnp.float32)
    end = jnp.zeros((kept.shape[0] - 2 * rows - BLOCK, LANES), jnp.float32)
    overlap = dot_3(*in_order(my_tile[...], other_tile[...]), ((1,), (1,)))
    products = in_order(overlap[:, :LANES], overlap[:, LANES:])
    grads = (my_grad[...], dot_3(residual[...], other_tile[...], ((1,), (1,))))
    for i, (out, grad) in enumerate(zip((kept, sent), grads)):
        out[:classes, :] = grad[:, :LANES]
        out[classes:rows, :] = gap
        out[rows : rows + classes, :] = grad[:, LANES:]
        out[rows + classes : 2 * rows, :] = gap
        out[2 * rows : 2 * rows + BLOCK, :] = products[i]
        out[2 * rows + BLOCK :, :] = end


def make_products(my_tile, my_grad, other, points, residual):
    half = jax.ShapeDtypeStruct((up(2 * up(residual.shape[0], 8) + BLOCK, 128), LANES), jnp.float32)
    return pl.pallas_call(
        products_kernel,
        out_shape=(jax.ShapeDtypeStruct(my_tile.shape, jnp.float32), half, half),
        in_specs=[VMEM] * 5,
        out_specs=(VMEM,) * 3,
        name="products",
        compiler_params=params(),
    )(my_tile, my_grad, other, points, residual)


def gram_kernel(features, mine, gram):
    block = block_of(mine, features)
    diagonal = lax.broadcasted_iota(jnp.int32, gram.shape, 0) == lax.broadcasted_iota(jnp.int32, gram.shape, 1)
    gram[...] = kernel_values(block, block) + jnp.where(diagonal, ridge, 0.0)


def make_gram(mine, features):
    return pl.pallas_call(
        functools.partial(gram_kernel, features),
        out_shape=jax.ShapeDtypeStruct((BLOCK, BLOCK), jnp.float32),
        in_specs=[VMEM],
        out_specs=VMEM,
        name="gram",
        compiler_params=params(),
        cost_estimate=pl.CostEstimate(flops=SWEEP_FLOPS // 4, bytes_accessed=1 << 20, transcendentals=0),
    )(mine)


def inverse_2(a, b, d):
    r = 1.0 / (a * d - b * b)
    return d * r, -b * r, a * r


def inverse_4(v):
    pair = range(2)
    x, y, z = inverse_2(v[0][0], v[0][1], v[1][1])
    corner = [[x, y], [y, z]]
    right = [[v[i][2 + j] for j in pair] for i in pair]
    u = [[corner[i][0] * right[0][j] + corner[i][1] * right[1][j] for j in pair] for i in pair]
    rest = [[v[2 + i][2 + j] - (right[0][i] * u[0][j] + right[1][i] * u[1][j]) for j in pair] for i in pair]
    e, f, g = inverse_2(rest[0][0], rest[0][1], rest[1][1])
    last = [[e, f], [f, g]]
    w = [[u[i][0] * last[0][j] + u[i][1] * last[1][j] for j in pair] for i in pair]
    first = [[corner[i][j] + w[i][0] * u[j][0] + w[i][1] * u[j][1] for j in pair] for i in pair]
    return [
        [first[0][0], first[0][1], -w[0][0], -w[0][1]],
        [first[0][1], first[1][1], -w[1][0], -w[1][1]],
        [-w[0][0], -w[1][0], e, f],
        [-w[0][1], -w[1][1], f, g],
    ]


def negative_inverse(p):
    n = p.shape[0]
    down = lax.broadcasted_iota(jnp.int32, (n, n), 0)
    along = lax.broadcasted_iota(jnp.int32, (n, n), 1)
    four = range(4)
    for j in range(0, n, 4):
        cols = [jnp.broadcast_to(p[:, j + i : j + i + 1], (n, n)) for i in four]
        rows = [p[j + i : j + i + 1, :] for i in four]
        w = inverse_4([[cols[k][j + i : j + i + 1, :] for k in four] for i in four])
        past = (along[:1] >= j) & (along[:1] < j + 4)
        rows = [jnp.where(past, 0.0, row) for row in rows]
        scaled = [sum(w[i][k] * rows[k] for k in four) for i in four]
        for i in four:
            p = p - cols[i] * scaled[i]
        for k in four:
            fresh = sum(cols[i] * w[i][k] for i in four)
            p = jnp.where(along == j + k, fresh, p)
        for i in four:
            row = scaled[i]
            for k in four:
                row = jnp.where(along[:1] == j + k, -w[i][k], row)
            p = jnp.where(down == j + i, row, p)
    return p


def sweep_kernel(spans, source, out):
    n = out.shape[1]
    for at, size in spans:
        along = lax.broadcasted_iota(jnp.int32, (size, n), 1)
        past = (along >= at) & (along < at + size)
        rows = source[at : at + size, :]
        pivot = negative_inverse(rows[:, at : at + size])
        panel = jnp.where(past, 0.0, rows)
        scaled = dot(pivot, panel, ((1,), (0,)))
        wide = jnp.pad(pivot, ((0, 0), (at, n - at - size)))
        fresh = jnp.where(past, wide, -scaled)
        out[...] = source[...] + dot(panel, scaled, ((0,), (0,)))
        out[at : at + size, :] = fresh
        out[:, at : at + size] = fresh.T
        source = out


def sweep(gram, *spans):
    return pl.pallas_call(
        functools.partial(sweep_kernel, spans),
        out_shape=jax.ShapeDtypeStruct(gram.shape, gram.dtype),
        in_specs=[VMEM],
        out_specs=VMEM,
        name="sweep",
        compiler_params=params(),
        cost_estimate=pl.CostEstimate(flops=SWEEP_FLOPS * sum(size for _, size in spans) // 64, bytes_accessed=1 << 20, transcendentals=0),
    )(gram)


def finish_kernel(
    places, my_sums, other_sums, my_inverse, other_inverse, my_tile, other_tile, residual, coeffs, new_residual, new_coeffs
):
    here = lax.axis_index(AXES)
    classes, width = residual.shape
    rows = up(classes, 8)
    sums = in_order(my_sums[...], other_sums[...])
    inverses = in_order(my_inverse[...], other_inverse[...])
    grads = [jnp.concatenate([half[:rows, :], half[rows : 2 * rows, :]], axis=1) for half in sums]
    overlap = jnp.concatenate([half[2 * rows : 2 * rows + BLOCK, :] for half in sums], axis=1)

    def direction(grad, inverse):
        scale = step_norm / jnp.sqrt(jnp.sum(grad * grad) * (1.0 / (classes * BLOCK)) + 1e-06)
        return dot_3(grad, inverse, ((1,), (0,))) * -scale

    delta0 = direction(grads[0], inverses[0])
    delta1 = direction(grads[1] - dot_3(delta0, overlap, ((1,), (0,))), inverses[1])
    deltas = [delta[:classes] for delta in (delta0, delta1)]
    tiles = in_order(my_tile[...], other_tile[...])
    after0 = residual[...] - dot_3(deltas[0], tiles[0], ((1,), (0,)))
    new_residual[...] = after0 - dot_3(deltas[1], tiles[1], ((1,), (0,)))
    new_coeffs[...] = coeffs[...]
    for step in range(2):

        @pl.when(places[0, step] == here)
        def _():
            wide = jnp.concatenate([deltas[step], jnp.zeros((classes, width - BLOCK), jnp.float32)], axis=1)
            new_coeffs[...] = new_coeffs[...] + pltpu.roll(wide, places[1, step], axis=1)


def finish(places, *arrays):
    residual, coeffs = arrays[-2:]
    return pl.pallas_call(
        finish_kernel,
        out_shape=(jax.ShapeDtypeStruct(residual.shape, jnp.float32), jax.ShapeDtypeStruct(coeffs.shape, jnp.float32)),
        in_specs=[SMEM] + [VMEM] * 8,
        out_specs=(VMEM, VMEM),
        name="finish",
        compiler_params=params(),
    )(places, *arrays)


def body(points, residual, coeffs, owners, offsets):
    places = jnp.stack([owners, offsets])
    mine, _ = all_reduce(*stage(places, points))
    other, (my_tile, my_grad) = lax.optimization_barrier((swap(mine), make_tile(mine, points, residual)))
    other_tile, kept, sent = make_products(my_tile, my_grad, other, points, residual)
    gram = make_gram(mine, points.shape[0])

    def last(gram):
        inverse = sweep(gram, (192, 64))
        return inverse, swap(inverse)

    sums, inverses = all_reduce(kept, sent, (lambda _: sweep(gram, (0, 64), (64, 32)), lambda m: sweep(m, (96, 32), (128, 64)), last))
    return finish(places, sums, swap(sums), *inverses, my_tile, other_tile, residual, coeffs)


def solution(mesh):
    split = P(None, AXES)
    return jax.shard_map(
        body,
        mesh=mesh,
        in_specs=(split, split, split, P(), P()),
        out_specs=(split, split),
        check_vma=False,
    )
```
